32 devices in a mesh: gx: 4 (over z), gy: 8 (over y, x, core).
Axes of the slice: x: 2, y: 2, z: 4, core: 2. Of those that a mesh axis runs over, the one named last changes fastest.
Arguments:
- velocity: float32 [3, 64, 256, 512], P(None, None, 'gy', 'gx'), may hold values from -6 to 6
- pressure: float32 [64, 256, 512], P(None, 'gy', 'gx'), may hold values from -6 to 6
- memory: float32 [64, 256, 512], P(None, 'gy', 'gx'), may hold values from -4 to 4
- buoyancy: float32 [64, 256, 512], P(None, 'gy', 'gx'), may hold values from 0.1 to 0.4
- modulus: float32 [64, 256, 512], P(None, 'gy', 'gx'), may hold values from 0.1 to 0.4
- relax: float32 [64, 256, 512], P(None, 'gy', 'gx'), may hold values from 0.05 to 0.5
- strength: float32 [64, 256, 512], P(None, 'gy', 'gx'), may hold values from 0.2 to 1
- spectra: float32 [2048, 256], P(('gx', 'gy')), may hold values from -6 to 6
- patch_cell: int32 [2048], P(('gx', 'gy')), may hold values from 0 to 262143
- rupture_patches: int32 [32, 64], replicated, may hold values from -1 to 2047, as said below
- slip_weights: bfloat16 [32, 64, 512], P('gx', 'gy'), may hold values from -1 to 1
Outputs:
- velocity_out: float32 [3, 64, 256, 512], P(None, None, 'gy', 'gx')
- pressure_out: float32 [64, 256, 512], P(None, 'gy', 'gx')
- memory_out: float32 [64, 256, 512], P(None, 'gy', 'gx')
- spectra_out: float32 [2048, 256], P(('gx', 'gy'))
- slip_response: float32 [32, 512, 256], P('gx', 'gy')
The draws below stay inside these ranges and needn't reach their ends.
Inputs may be any that keep to these rules, and one draw needn't show every extreme that they name: `patch_cell`: the cell of a patch is a flat index (z * 32 + y) * 128 + x within its brick. `rupture_patches`: each patch is listed in at most one slot. Slot (r, s) belongs to the owner at index r // 8 of gx and s // 8 of gy; of the 64 patches of one block, at most 2 are listed in the slots of any one owner, and some pairs of block and owner reach 2.
All inputs are finite; a program needn't handle non-finite values.
Results may differ from the reference program's by a relative error of at most 0.0029.
Values may be sent and summed in bfloat16 or wider, within the bound.
A program may use at most 128 MiB of HBM per device.

```python
import math
import jax
import jax.numpy as jnp
from jax import lax

CX = 128
CY = 32
CZ = 64
STEPS = 4
FREQS = 128
VARS = 512
CAP = 2
RUP_GROUP = 8
PATCH_DEV = 64
NX = 512
NY = 256
PATCHES = 2048
SLOT_DEV = 8
SLOTS = 64
RUPTURES = 32
N_GY = 8


def draw_rupture_patches(key, part):
    devs = PATCHES // PATCH_DEV
    groups_y = SLOTS // SLOT_DEV
    keys = jax.random.split(jax.random.fold_in(key, 7), 7)
    sigma = jax.random.permutation(keys[0], devs)
    tau = jax.random.permutation(keys[1], devs)
    offsets = jax.random.permutation(keys[2], devs)[:PATCH_DEV // CAP]
    position = jnp.arange(PATCH_DEV, dtype=jnp.int32)
    group_of = position // CAP
    target = sigma[(tau[:, None] + offsets[None, :]) % devs]
    target_pos = target[:, group_of]
    order = jax.vmap(lambda k: jax.random.permutation(k, PATCH_DEV))(jax.random.split(keys[3], devs))
    patch_global = jnp.arange(devs, dtype=jnp.int32)[:, None] * PATCH_DEV + order.astype(jnp.int32)
    slot_perm = jax.vmap(lambda k: jax.random.permutation(k, PATCH_DEV))(jax.random.split(keys[4], devs))
    local = slot_perm[target_pos, position[None, :]]
    levels = jnp.array([100, 100, 100, 50], dtype=jnp.int32)
    heat = levels[jax.random.randint(keys[5], (devs,), 0, 4)]
    heat = heat.at[sigma[0]].set(100)
    keep = jax.random.randint(keys[6], (devs, PATCH_DEV), 0, 100) < heat[target_pos]
    row = target_pos // groups_y * RUP_GROUP + local // SLOT_DEV
    col = target_pos % groups_y * SLOT_DEV + local % SLOT_DEV
    flat = row * SLOTS + col
    total = RUPTURES * SLOTS
    table = jnp.full((total + 1,), -1, dtype=jnp.int32)
    table = table.at[jnp.where(keep, flat, total).reshape(-1)].set(patch_global.reshape(-1))
    return table[:total].reshape(RUPTURES, SLOTS)


def place_ends(values, own_key, least, top_value):
    place = [jax.random.randint(jax.random.fold_in(own_key, axis), (), 0, length) for axis, length in enumerate(values.shape)]
    longest = values.shape.index(max(values.shape))
    neighbour = place[:longest] + [(place[longest] + 1) % values.shape[longest]] + place[longest + 1:]
    return values.at[tuple(place)].set(least).at[tuple(neighbour)].set(top_value)


def with_spikes(values, own_key, source, target, parts, factor):
    owner, partner = [(jnp.arange(values.shape[dim]) // (values.shape[dim] // parts)).reshape([-1 if axis == dim else 1 for axis in range(values.ndim)]) for dim in (source, target)]
    chosen = jax.random.permutation(own_key, parts)[partner]
    strong = (owner == chosen) | (owner == (partner + parts // 2) % parts)
    return jnp.where(strong, factor * values, values)


def block_levels(key, shape, cuts, least, largest):
    level = 1.0
    for dim, shards_of in cuts:
        heights = jax.random.uniform(jax.random.fold_in(jax.random.fold_in(key, 6), dim), (shards_of,), jnp.float32, least / len(cuts), largest / len(cuts))
        level = level * jnp.repeat(jnp.exp(heights), shape[dim] // shards_of).reshape((-1,) + (1,) * (len(shape) - 1 - dim))
    return level


def scatter_about(own_key, shape, scale, reach, pieces=(), kind=jnp.bfloat16):
    values = jax.random.normal(own_key, shape, jnp.float32) * scale
    if len(pieces) > 0:
        values = block_levels(own_key, shape, pieces, -0.22, 0.18) * values
    return jnp.clip(values, min=-reach, max=reach).astype(kind)


def noise_with(rng, dims, scale, bound, cuts, heavy, kind=jnp.bfloat16):
    values = scale * jax.random.normal(rng, dims, jnp.float32)
    if cuts:
        values = values * block_levels(rng, dims, cuts, -0.22, 0.18)
    return jnp.clip(with_spikes(values, jax.random.fold_in(rng, 3), *heavy), -bound, bound).astype(kind)


def setup_inputs(seed: int = 0) -> dict:
    splits = jax.random.split(jax.random.key(seed), 12)
    velocity = scatter_about(splits[0], (3, CZ, NY, NX), 1.0, 6.0, ((2, 8), (3, 4)), jnp.float32)
    pressure = scatter_about(splits[1], (CZ, NY, NX), 1.0, 6.0, ((1, 8), (2, 4)), jnp.float32)
    memory = scatter_about(splits[2], (CZ, NY, NX), 0.3, 4.0, ((1, 8), (2, 4)), jnp.float32)
    buoyancy = jnp.clip(jnp.exp(math.log(0.4) - 1.3862944 * jax.random.uniform(splits[3], (CZ, NY, NX), jnp.float32) ** block_levels(splits[3], (CZ, NY, NX), ((1, 8), (2, 4)), -0.2, 0.2)), 0.1, 0.4)
    modulus = jnp.clip(jnp.exp(math.log(0.4) - 1.3862944 * jax.random.uniform(splits[4], (CZ, NY, NX), jnp.float32) ** block_levels(splits[4], (CZ, NY, NX), ((1, 8), (2, 4)), -0.2, 0.2)), 0.1, 0.4)
    relax = jnp.clip(jnp.exp(math.log(0.5) - 2.3025851 * jax.random.uniform(splits[5], (CZ, NY, NX), jnp.float32) ** block_levels(splits[5], (CZ, NY, NX), ((1, 8), (2, 4)), -0.2, 0.2)), 0.05, 0.5)
    strength = jnp.clip(0.2 + 0.8 * jax.random.uniform(splits[6], (CZ, NY, NX), jnp.float32) ** block_levels(splits[6], (CZ, NY, NX), ((1, 8), (2, 4)), -0.2, 0.2), 0.2, 1.0)
    spectra = scatter_about(splits[7], (PATCHES, 2 * FREQS), 1.0, 6.0, ((0, 32),), jnp.float32)
    patch_cell = place_ends(jax.random.randint(splits[8], (PATCHES,), 0, CX * CY * CZ), jax.random.fold_in(splits[8], 1), 0, (CX * CY * CZ) - 1).astype(jnp.int32)
    rupture_patches = draw_rupture_patches(jax.random.fold_in(splits[11], 71), 0)
    slip_weights = noise_with(splits[10], (RUPTURES, SLOTS, VARS), SLOTS ** -0.5, 1.0, ((0, 4), (1, 8)), (1, 2, 8, 2.0))
    return {"velocity": velocity, "pressure": pressure, "memory": memory, "buoyancy": buoyancy, "modulus": modulus, "relax": relax, "strength": strength, "spectra": spectra, "patch_cell": patch_cell, "rupture_patches": rupture_patches, "slip_weights": slip_weights}


def centred(field, axis):
    widths = [(0, 0), (0, 0), (0, 0)]
    widths[axis] = (1, 1)
    padded = jnp.pad(field, widths)
    length = field.shape[axis]
    return lax.slice_in_dim(padded, 2, length + 2, axis=axis) - lax.slice_in_dim(padded, 0, length, axis=axis)


def phase_row(freqs, step):
    angle = jnp.pi * (jnp.arange(freqs, dtype=jnp.float32) + 0.5) / freqs * step
    return jnp.concatenate([jnp.cos(angle), -jnp.sin(angle)])


def reference(velocity, pressure, memory, buoyancy, modulus, relax, strength, spectra, patch_cell, rupture_patches, slip_weights):
    speed_x, speed_y, speed_z = velocity[0], velocity[1], velocity[2]
    freqs = spectra.shape[1] // 2
    block = jnp.arange(spectra.shape[0], dtype=jnp.int32) // PATCH_DEV
    col_block = block // N_GY
    row_block = block % N_GY
    depth = patch_cell // (CY * CX)
    rows = row_block * CY + (patch_cell // CX) % CY
    cols = col_block * CX + patch_cell % CX
    for step in range(STEPS):
        speed_x = speed_x - buoyancy * centred(pressure, 2)
        speed_y = speed_y - buoyancy * centred(pressure, 1)
        speed_z = speed_z - buoyancy * centred(pressure, 0)
        spread = centred(speed_x, 2) + centred(speed_y, 1) + centred(speed_z, 0)
        shear = centred(speed_x, 1) + centred(speed_y, 2)
        memory = memory - relax * (memory + strength * spread)
        pressure = pressure - modulus * (spread + memory)
        sample = shear[depth, rows, cols]
        spectra = spectra + sample[:, None] * phase_row(freqs, step + 1)[None, :]
    live = rupture_patches >= 0
    picked = spectra[jnp.where(live, rupture_patches, 0)]
    slot_spectra = jnp.where(live[:, :, None], picked, jnp.zeros_like(picked)).astype(jnp.bfloat16)
    slip = jnp.einsum("rsv,rsf->rvf", slip_weights.astype(jnp.float32), slot_spectra.astype(jnp.float32))
    velocity_out = jnp.stack([speed_x, speed_y, speed_z])
    return velocity_out, pressure, memory, spectra, slip
```

```python
import functools

import jax
import jax.numpy as jnp
from jax import lax
from jax.experimental import pallas as pl
from jax.experimental.pallas import tpu as pltpu
from jax.sharding import PartitionSpec as P

STEPS = 4
CAP = 2
BATCH = 4


def phase_row(freqs, step):
    angle = jnp.pi * (jnp.arange(freqs, dtype=jnp.float32) + 0.5) / freqs * step
    return jnp.concatenate([jnp.cos(angle), -jnp.sin(angle)])


Y_ROWS = [4] + [3] * (STEPS - 1) + [1]
X_PACKS = [3] + [2] * (STEPS - 1) + [1]


def step_kernel(dims, *refs):
    nz, ny, nx, chunks, zc, per_dev, ngx, ngy = dims
    refs = list(refs)
    take = lambda count: [refs.pop(0) for _ in range(count)]
    vel_in, p_in, m_in, b_in, mod_in, rel_in, str_in, spectra, cell, cell_col, phase = take(11)
    vel_out, p_out, m_out, spectra_out = take(4)
    vx, vy, vz, p, m, b, mod, rel, stg = take(9)
    ysend, yrecv = (take(STEPS + 1), take(STEPS + 1))
    xsend, xrecv = (take(STEPS + 1), take(STEPS + 1))
    vxh, bxh, hx, vyh, rows_got, samples = take(6)
    in_sem, out_sem, send_sem, recv_sem = take(4)

    gx, gy = (lax.axis_index("gx"), lax.axis_index("gy"))
    has = [gy > 0, gy < ngy - 1, gx > 0, gx < ngx - 1]
    peer = [{"gy": gy - 1}, {"gy": gy + 1}, {"gx": gx - 1}, {"gx": gx + 1}]

    loads = [
        pltpu.make_async_copy(src, dst, in_sem.at[i])
        for i, (src, dst) in enumerate(
            [
                (p_in, p.at[pl.ds(1, nz)]),
                (b_in, b.at[pl.ds(0, nz)]),
                (vel_in.at[0], vx),
                (vel_in.at[1], vy),
                (vel_in.at[2], vz.at[pl.ds(1, nz)]),
                (rel_in, rel),
                (m_in, m),
                (str_in, stg),
                (mod_in, mod),
            ]
        )
    ]
    for load in loads:
        load.start()

    barrier = pltpu.get_barrier_semaphore()
    for side in range(4):

        @pl.when(has[side])
        def _():
            pl.semaphore_signal(
                barrier, inc=1, device_id=peer[side], device_id_type=pl.DeviceIdType.MESH
            )

    plane = jnp.zeros((ny, nx), jnp.float32)
    p[0] = plane
    p[nz + 1] = plane
    p[nz + 2] = plane
    vz[0] = plane
    vz[nz + 1] = plane
    b[nz] = plane
    for side in range(4):

        @pl.when(jnp.logical_not(has[side]))
        def _():
            for r in range(STEPS + 1):
                if side < 2:
                    yrecv[r][side] = jnp.zeros(yrecv[r].shape[1:], jnp.float32)
                else:
                    xrecv[r][side - 2] = jnp.zeros(xrecv[r].shape[1:], jnp.float32)

    def copy_to(r, c, side):
        slot = side % 2
        if side < 2:
            src, dst = (ysend[r].at[slot, c], yrecv[r].at[1 - slot, c])
        else:
            src, dst = (xsend[r].at[c], xrecv[r].at[1 - slot, c])
        return pltpu.make_async_remote_copy(
            src_ref=src,
            dst_ref=dst,
            send_sem=send_sem.at[r, c, side],
            recv_sem=recv_sem.at[r, c, side - side % 2 + 1 - slot],
            device_id=peer[side],
            device_id_type=pl.DeviceIdType.MESH,
        )

    def copy_from(r, c, side):
        slot = side % 2
        if side < 2:
            src, dst = (ysend[r].at[slot, c], yrecv[r].at[slot, c])
        else:
            src, dst = (xsend[r].at[c], xrecv[r].at[slot, c])
        return pltpu.make_async_remote_copy(
            src_ref=src,
            dst_ref=dst,
            send_sem=send_sem.at[r, c, side],
            recv_sem=recv_sem.at[r, c, side],
            device_id=peer[side],
            device_id_type=pl.DeviceIdType.MESH,
        )

    def send(r, c):
        for side in range(4):

            @pl.when(has[side])
            def _():
                copy_to(r, c, side).start()

    def receive(r, c):
        for side in range(4):

            @pl.when(has[side])
            def _():
                copy_from(r, c, side).wait_recv()

    lane = lax.broadcasted_iota(jnp.int32, (ny, nx), 1)
    row = lax.broadcasted_iota(jnp.int32, (ny, nx), 0)
    quad, lane4 = (lane // 4, lane % 4)
    last_lane, first_lane = (lane == nx - 1, lane == 0)
    last_row, first_row = (row == ny - 1, row == 0)

    def pack(total, slab, zl):
        return jnp.where(quad == zl, pltpu.roll(slab, 4 * zl + 2, 1), total)

    def d_x(slab, halo, zl):
        ends = pltpu.roll(halo, nx - 2 - 4 * zl, 1)
        after = jnp.where(last_lane, ends, pltpu.roll(slab, nx - 1, 1))
        before = jnp.where(first_lane, ends, pltpu.roll(slab, 1, 1))
        return after - before

    def d_y(slab, south, north):
        after = jnp.where(last_row, north, pltpu.roll(slab, ny - 1, 0))
        before = jnp.where(first_row, south, pltpu.roll(slab, 1, 0))
        return after - before

    for load in loads[:4]:
        load.wait()
    for c in range(chunks):

        def edges(i, totals):
            pt, vt, bt = totals
            for j in range(BATCH):
                zl = i * BATCH + j
                z = c * zc + zl
                ps, vs, ws, bs = (p[z + 1], vx[z], vy[z], b[z])
                pt, vt, bt = (pack(pt, ps, zl), pack(vt, vs, zl), pack(bt, bs, zl))
                at = pl.ds(zl, 1)
                ysend[0][0, c, 0, at, :] = ps[0:1]
                ysend[0][0, c, 1, at, :] = ps[1:2]
                ysend[0][0, c, 2, at, :] = ws[0:1]
                ysend[0][0, c, 3, at, :] = bs[0:1]
                ysend[0][1, c, 0, at, :] = ps[ny - 2 : ny - 1]
                ysend[0][1, c, 1, at, :] = ps[ny - 1 : ny]
                ysend[0][1, c, 2, at, :] = ws[ny - 1 : ny]
                ysend[0][1, c, 3, at, :] = bs[ny - 1 : ny]
            return pt, vt, bt

        totals = lax.fori_loop(0, zc // BATCH, edges, (plane, plane, plane))
        for i, total in enumerate(totals):
            xsend[0][c, i] = total
        if c == 0:
            pl.semaphore_wait(barrier, sum(side.astype(jnp.int32) for side in has))
        send(0, c)
    for load in loads[4:]:
        load.wait()

    def halos(r, c):
        def joined(i):
            return jnp.where(lane4 < 2, xrecv[r][0, c, i], xrecv[r][1, c, i])

        def swapped(halo):
            return jnp.where(lane4 == 1, pltpu.roll(halo, nx - 1, 1), pltpu.roll(halo, 1, 1))

        outer, own = (joined(0), xsend[r][c, 0])
        if r == 0:
            vh, bh = (joined(1), joined(2))
            bxh[c] = bh
            vyh[0, c] = yrecv[0][0, c, 2]
            vyh[1, c] = yrecv[0][1, c, 2]
        else:
            vh, bh = (vxh[c], bxh[c])
        slope = jnp.where(
            lane4 == 1,
            pltpu.roll(own, nx - 1, 1) - pltpu.roll(outer, 1, 1),
            pltpu.roll(outer, nx - 1, 1) - pltpu.roll(own, 1, 1),
        )
        vh = vh - bh * slope
        vxh[c] = vh
        hx[0, c] = swapped(outer)
        hx[1, c] = swapped(vh)
        vyh[0, c] = vyh[0, c] - yrecv[0][0, c, 3] * (ysend[r][0, c, 0] - yrecv[r][0, c, 0])
        vyh[1, c] = vyh[1, c] - yrecv[0][1, c, 3] * (yrecv[r][1, c, 1] - ysend[r][1, c, 1])

    def sweep(r, c):
        last = r == STEPS - 1
        n = r + 1

        def body(i, totals):
            pt, wt = totals
            base = i * BATCH
            z0 = c * zc + base
            ps = [p[z0 + 1 + j] for j in range(BATCH + 2)]
            bs = [b[z0 + j] for j in range(BATCH + 1)]
            zs = [vz[z0], vz[z0 + 1]]
            vs, ws, new_p = ([], [], [])
            for j in range(BATCH):
                zl = base + j
                at = pl.ds(zl, 1)
                zs.append(vz[z0 + j + 2] - bs[j + 1] * (ps[j + 2] - ps[j]))
                vs.append(vx[z0 + j] - bs[j] * d_x(ps[j], hx[0, c], zl))
                south, north = (yrecv[r][0, c, 1, at, :], yrecv[r][1, c, 0, at, :])
                ws.append(vy[z0 + j] - bs[j] * d_y(ps[j], south, north))
            for j in range(BATCH):
                zl = base + j
                at = pl.ds(zl, 1)
                spread = d_x(vs[j], hx[1, c], zl) + d_y(ws[j], vyh[0, c, at, :], vyh[1, c, at, :])
                spread = spread + (zs[j + 2] - zs[j])
                mem = m[z0 + j]
                mem = mem - rel[z0 + j] * (mem + stg[z0 + j] * spread)
                m[z0 + j] = mem
                new_p.append(ps[j] - mod[z0 + j] * (spread + mem))
            for j in range(BATCH):
                zl = base + j
                at = pl.ds(zl, 1)
                vz[z0 + j + 2] = zs[j + 2]
                vx[z0 + j] = vs[j]
                vy[z0 + j] = ws[j]
                p[z0 + j + 1] = new_p[j]
                wt = pack(wt, ws[j], zl)
                ysend[n][0, c, 0 if last else 2, at, :] = vs[j][0:1]
                ysend[n][1, c, 0 if last else 2, at, :] = vs[j][ny - 1 : ny]
                if not last:
                    pt = pack(pt, new_p[j], zl)
                    ysend[n][0, c, 0, at, :] = new_p[j][0:1]
                    ysend[n][0, c, 1, at, :] = new_p[j][1:2]
                    ysend[n][1, c, 0, at, :] = new_p[j][ny - 2 : ny - 1]
                    ysend[n][1, c, 1, at, :] = new_p[j][ny - 1 : ny]
            return pt, wt

        pt, wt = lax.fori_loop(0, zc // BATCH, body, (plane, plane))
        if last:
            xsend[n][c, 0] = wt
        else:
            xsend[n][c, 0] = pt
            xsend[n][c, 1] = wt

    cells = cell_col[...]
    cell_z, cell_y, cell_x = (cells // (ny * nx), (cells // nx) % ny, cells % nx)
    patch_lane = lax.broadcasted_iota(jnp.int32, (per_dev, nx), 1)

    def masked(keep, values):
        return jnp.where(keep, values, 0.0)

    def sample_own(n):
        def body(i, carry):
            at = cell[i]
            z, y = (at // (ny * nx), (at // nx) % ny)
            out = pl.ds(i, 1)
            rows_got[0, out, :] = vx[z, pl.ds(jnp.minimum(y + 1, ny - 1), 1), :]
            rows_got[1, out, :] = vx[z, pl.ds(jnp.maximum(y - 1, 0), 1), :]
            rows_got[2, out, :] = vy[z, pl.ds(y, 1), :]
            return carry

        lax.fori_loop(0, per_dev, body, 0, unroll=8)
        along = masked(cell_y < ny - 1, rows_got[0]) - masked(cell_y > 0, rows_got[1])
        across = rows_got[2]
        total = masked(patch_lane == cell_x, along)
        total = total + masked(patch_lane == cell_x + 1, across)
        samples[n - 1] = total - masked(patch_lane == cell_x - 1, across)

    def sample_halo(n):
        which_row, which_pack = (Y_ROWS[n] - 1, X_PACKS[n] - 1)

        def body(i, carry):
            at = cell[i]
            z, y = (at // (ny * nx), (at // nx) % ny)
            c, zl = (z // zc, z % zc)
            out = pl.ds(i, 1)
            rows_got[0, out, :] = yrecv[n][0, c, which_row, pl.ds(zl, 1), :]
            rows_got[1, out, :] = yrecv[n][1, c, which_row, pl.ds(zl, 1), :]
            rows_got[2, out, :] = xrecv[n][0, c, which_pack, pl.ds(y, 1), :]
            rows_got[3, out, :] = xrecv[n][1, c, which_pack, pl.ds(y, 1), :]
            return carry

        lax.fori_loop(0, per_dev, body, 0, unroll=8)
        start = 4 * (cell_z % zc)
        here = patch_lane == cell_x
        total = samples[n - 1]
        total = total + masked(here & (cell_y == ny - 1), rows_got[1])
        total = total - masked(here & (cell_y == 0), rows_got[0])
        total = total + masked((patch_lane == start + 2) & (cell_x == nx - 1), rows_got[3])
        total = total - masked((patch_lane == start + 1) & (cell_x == 0), rows_got[2])
        value = jnp.sum(total, axis=1, keepdims=True)
        spectra_out[...] = spectra_out[...] + value * phase[n - 1 : n, :]

    spectra_out[...] = spectra[...]
    stores = []
    for r in range(STEPS):
        vz[1] = vz[1] - b[0] * (p[2] - p[0])
        for c in range(chunks):
            receive(r, c)
            halos(r, c)
            sweep(r, c)
            send(r + 1, c)
            if r == STEPS - 1:
                at = pl.ds(c * zc, zc)
                pairs = [
                    (vx.at[at], vel_out.at[0, at]),
                    (vy.at[at], vel_out.at[1, at]),
                    (vz.at[pl.ds(1 + c * zc, zc)], vel_out.at[2, at]),
                    (p.at[pl.ds(1 + c * zc, zc)], p_out.at[at]),
                    (m.at[at], m_out.at[at]),
                ]
                for i, (src, dst) in enumerate(pairs):
                    store = pltpu.make_async_copy(src, dst, out_sem.at[c, i])
                    store.start()
                    stores.append(store)
        sample_own(r + 1)
        if r > 0:
            sample_halo(r)
    for c in range(chunks):
        receive(STEPS, c)
    sample_halo(STEPS)
    for r in range(STEPS + 1):
        for c in range(chunks):
            for side in range(4):

                @pl.when(has[side])
                def _():
                    copy_to(r, c, side).wait_send()

    for store in stores:
        store.wait()


def advance(velocity, pressure, memory, buoyancy, modulus, relax, strength, spectra, patch_cell):
    nz, ny, nx = pressure.shape
    per_dev, width = spectra.shape
    zc = nx // 4
    chunks = nz // zc
    dims = (nz, ny, nx, chunks, zc, per_dev, lax.axis_size("gx"), lax.axis_size("gy"))
    phase = jnp.stack([phase_row(width // 2, n + 1) for n in range(STEPS)])
    f32 = jnp.float32
    field = lambda planes: pltpu.VMEM((planes, ny, nx), f32)
    rounds = range(STEPS + 1)
    any_spec = pl.BlockSpec(memory_space=pl.ANY)
    vmem_spec = pl.BlockSpec(memory_space=pltpu.VMEM)
    return pl.pallas_call(
        functools.partial(step_kernel, dims),
        out_shape=[
            jax.ShapeDtypeStruct(velocity.shape, f32),
            jax.ShapeDtypeStruct(pressure.shape, f32),
            jax.ShapeDtypeStruct(memory.shape, f32),
            jax.ShapeDtypeStruct(spectra.shape, f32),
        ],
        in_specs=[any_spec] * 7
        + [vmem_spec, pl.BlockSpec(memory_space=pltpu.SMEM), vmem_spec, vmem_spec],
        out_specs=[any_spec] * 3 + [vmem_spec],
        scratch_shapes=[field(nz), field(nz), field(nz + 2), field(nz + 3), field(nz)]
        + [field(nz + 1), field(nz), field(nz), field(nz)]
        + [pltpu.VMEM((2, chunks, Y_ROWS[r], zc, nx), f32) for r in rounds]
        + [pltpu.VMEM((2, chunks, Y_ROWS[r], zc, nx), f32) for r in rounds]
        + [pltpu.VMEM((chunks, X_PACKS[r], ny, nx), f32) for r in rounds]
        + [pltpu.VMEM((2, chunks, X_PACKS[r], ny, nx), f32) for r in rounds]
        + [
            pltpu.VMEM((chunks, ny, nx), f32),
            pltpu.VMEM((chunks, ny, nx), f32),
            pltpu.VMEM((2, chunks, ny, nx), f32),
            pltpu.VMEM((2, chunks, zc, nx), f32),
            pltpu.VMEM((4, per_dev, nx), f32),
            pltpu.VMEM((STEPS, per_dev, nx), f32),
            pltpu.SemaphoreType.DMA((9,)),
            pltpu.SemaphoreType.DMA((chunks, 5)),
            pltpu.SemaphoreType.DMA((STEPS + 1, chunks, 4)),
            pltpu.SemaphoreType.DMA((STEPS + 1, chunks, 4)),
        ],
        compiler_params=pltpu.CompilerParams(collective_id=0, has_side_effects=True),
    )(
        velocity,
        pressure,
        memory,
        buoyancy,
        modulus,
        relax,
        strength,
        spectra,
        patch_cell,
        patch_cell.reshape(-1, 1),
        phase,
    )


def per_device(
    velocity,
    pressure,
    memory,
    buoyancy,
    modulus,
    relax,
    strength,
    spectra,
    patch_cell,
    rupture_patches,
    slip_weights,
):
    velocity_out, pressure, memory, spectra = advance(
        velocity, pressure, memory, buoyancy, modulus, relax, strength, spectra, patch_cell
    )
    freqs = spectra.shape[1] // 2
    groups_x = lax.axis_size("gx")
    groups_y = lax.axis_size("gy")
    devices = groups_x * groups_y
    owner = lax.axis_index("gx") * groups_y + lax.axis_index("gy")
    per_dev = spectra.shape[0]
    rup_group, slot_dev, variations = slip_weights.shape
    slots = rupture_patches.shape[1]
    flat_ids = rupture_patches.reshape(-1)
    slot_index = jnp.arange(flat_ids.shape[0], dtype=jnp.int32)
    target = slot_index // slots // rup_group * groups_y + slot_index % slots // slot_dev
    own_ids = owner * per_dev + jnp.arange(per_dev, dtype=jnp.int32)
    matches = flat_ids[None, :] == own_ids[:, None]
    target_of = jnp.max(jnp.where(matches, target[None, :], -1), axis=1)
    counter = jnp.arange(per_dev, dtype=jnp.int32)
    before = counter[None, :] < counter[:, None]
    rank = jnp.sum(((target_of[None, :] == target_of[:, None]) & before).astype(jnp.int32), axis=1)
    bucket = jnp.where(target_of >= 0, target_of * CAP + rank, -1)
    placing = (jnp.arange(devices * CAP, dtype=jnp.int32)[:, None] == bucket[None, :]).astype(
        jnp.bfloat16
    )
    rounded = spectra.astype(jnp.bfloat16)
    outgoing = jnp.dot(placing, rounded, preferred_element_type=jnp.float32).astype(jnp.bfloat16)
    outgoing = outgoing.reshape(devices, CAP, 2 * freqs)
    incoming = lax.all_to_all(outgoing, ("gx", "gy"), split_axis=0, concat_axis=0, tiled=True)
    received = incoming.reshape(devices * CAP, 2 * freqs)
    local_ids = lax.dynamic_slice(
        rupture_patches,
        (lax.axis_index("gx") * rup_group, lax.axis_index("gy") * slot_dev),
        (rup_group, slot_dev),
    ).reshape(-1)
    source = local_ids // per_dev
    earlier_slot = (
        (local_ids[None, :] < local_ids[:, None])
        & (source[None, :] == source[:, None])
        & (local_ids[None, :] >= 0)
    )
    rank_in = jnp.sum(earlier_slot.astype(jnp.int32), axis=1)
    live = local_ids >= 0
    row = jnp.where(live, source * CAP + rank_in, 0)
    picked = jnp.take(received, row, axis=0)
    slot_spectra = jnp.where(live[:, None], picked, jnp.zeros_like(picked)).reshape(
        rup_group, slot_dev, 2 * freqs
    )
    swapped = lax.all_to_all(slip_weights, "gy", split_axis=2, concat_axis=1, tiled=True)
    slip = jnp.einsum(
        "rsv,rsf->rvf",
        swapped,
        lax.all_gather(slot_spectra, "gy", axis=1, tiled=True),
        preferred_element_type=jnp.float32,
    )
    return (velocity_out, pressure, memory, spectra, slip)


def solution(mesh):
    in_specs = (
        P(None, None, "gy", "gx"),
        P(None, "gy", "gx"),
        P(None, "gy", "gx"),
        P(None, "gy", "gx"),
        P(None, "gy", "gx"),
        P(None, "gy", "gx"),
        P(None, "gy", "gx"),
        P(("gx", "gy"), None),
        P(("gx", "gy")),
        P(),
        P("gx", "gy", None),
    )
    out_specs = (
        P(None, None, "gy", "gx"),
        P(None, "gy", "gx"),
        P(None, "gy", "gx"),
        P(("gx", "gy"), None),
        P("gx", "gy", None),
    )
    return jax.shard_map(
        per_device, mesh=mesh, in_specs=in_specs, out_specs=out_specs, check_vma=False
    )
```

```python
import functools

import jax
import jax.numpy as jnp
import numpy as np
from jax import lax
from jax.experimental import pallas as pl
from jax.experimental.pallas import tpu as pltpu
from jax.sharding import PartitionSpec as P

STEPS = 4
CAP = 2
BATCH = 4


def phase_rows(freqs):
    angle = np.pi * (np.arange(freqs) + 0.5) / freqs
    rows = [np.concatenate([np.cos(angle * n), -np.sin(angle * n)]) for n in range(1, STEPS + 1)]
    return jnp.asarray(np.stack(rows).astype(np.float32))


Y_ROWS = [4] + [3] * (STEPS - 1) + [1]
X_PACKS = [3] + [2] * (STEPS - 1) + [1]


def step_kernel(dims, *refs):
    nz, ny, nx, chunks, zc, per_dev, ngx, ngy = dims
    refs = list(refs)
    take = lambda count: [refs.pop(0) for _ in range(count)]
    vel_in, p_in, m_in, b_in, mod_in, rel_in, str_in, spectra, cell, cell_row, phase = take(11)
    listed, weights = take(2)
    vel_out, p_out, m_out, spectra_out, weights_got, rows_out = take(6)
    vx, vy, vz, p, m, b, mod, rel, stg = take(9)
    ysend, yrecv = (take(STEPS + 1), take(STEPS + 1))
    xsend, xrecv = (take(STEPS + 1), take(STEPS + 1))
    vxh, bxh, hx, vyh, rows_got, samples = take(6)
    placing, rows_send, rows_group = take(3)
    in_sem, out_sem, send_sem, recv_sem, far_send, far_recv = take(6)

    gx, gy = (lax.axis_index("gx"), lax.axis_index("gy"))
    has = [gy > 0, gy < ngy - 1, gx > 0, gx < ngx - 1]
    peer = [{"gy": gy - 1}, {"gy": gy + 1}, {"gx": gx - 1}, {"gx": gx + 1}]

    loads = [
        pltpu.make_async_copy(src, dst, in_sem.at[i])
        for i, (src, dst) in enumerate(
            [
                (p_in, p.at[pl.ds(1, nz)]),
                (b_in, b.at[pl.ds(0, nz)]),
                (vel_in.at[0], vx),
                (vel_in.at[1], vy),
                (vel_in.at[2], vz.at[pl.ds(1, nz)]),
                (rel_in, rel),
                (m_in, m),
                (str_in, stg),
                (mod_in, mod),
            ]
        )
    ]
    for load in loads:
        load.start()

    along_gx = [lax.rem(gx + k, ngx) for k in range(1, ngx)]
    along_gy = [lax.rem(gy + k, ngy) for k in range(1, ngy)]
    peers = [{"gx": other} for other in along_gx] + [{"gy": other} for other in along_gy]
    barrier = pltpu.get_barrier_semaphore()
    for other in peers:
        pl.semaphore_signal(
            barrier, inc=1, device_id=other, device_id_type=pl.DeviceIdType.MESH
        )

    plane = jnp.zeros((ny, nx), jnp.float32)
    p[0] = plane
    p[nz + 1] = plane
    p[nz + 2] = plane
    vz[0] = plane
    vz[nz + 1] = plane
    b[nz] = plane
    for side in range(4):

        @pl.when(jnp.logical_not(has[side]))
        def _():
            for r in range(STEPS + 1):
                if side < 2:
                    yrecv[r][side] = jnp.zeros(yrecv[r].shape[1:], jnp.float32)
                else:
                    xrecv[r][side - 2] = jnp.zeros(xrecv[r].shape[1:], jnp.float32)

    def copy_to(r, c, side):
        slot = side % 2
        if side < 2:
            src, dst = (ysend[r].at[slot, c], yrecv[r].at[1 - slot, c])
        else:
            src, dst = (xsend[r].at[c], xrecv[r].at[1 - slot, c])
        return pltpu.make_async_remote_copy(
            src_ref=src,
            dst_ref=dst,
            send_sem=send_sem.at[r, c, side],
            recv_sem=recv_sem.at[r, c, side - side % 2 + 1 - slot],
            device_id=peer[side],
            device_id_type=pl.DeviceIdType.MESH,
        )

    def copy_from(r, c, side):
        slot = side % 2
        if side < 2:
            src, dst = (ysend[r].at[slot, c], yrecv[r].at[slot, c])
        else:
            src, dst = (xsend[r].at[c], xrecv[r].at[slot, c])
        return pltpu.make_async_remote_copy(
            src_ref=src,
            dst_ref=dst,
            send_sem=send_sem.at[r, c, side],
            recv_sem=recv_sem.at[r, c, side],
            device_id=peer[side],
            device_id_type=pl.DeviceIdType.MESH,
        )

    def send(r, c):
        for side in range(4):

            @pl.when(has[side])
            def _():
                copy_to(r, c, side).start()

    def receive(r, c):
        for side in range(4):

            @pl.when(has[side])
            def _():
                copy_from(r, c, side).wait_recv()

    lane = lax.broadcasted_iota(jnp.int32, (ny, nx), 1)
    row = lax.broadcasted_iota(jnp.int32, (ny, nx), 0)
    quad, lane4 = (lane // 4, lane % 4)
    last_lane, first_lane = (lane == nx - 1, lane == 0)
    last_row, first_row = (row == ny - 1, row == 0)

    def pack(total, slab, zl):
        return jnp.where(quad == zl, pltpu.roll(slab, 4 * zl + 2, 1), total)

    def d_x(slab, halo, zl):
        ends = pltpu.roll(halo, nx - 2 - 4 * zl, 1)
        after = jnp.where(last_lane, ends, pltpu.roll(slab, nx - 1, 1))
        before = jnp.where(first_lane, ends, pltpu.roll(slab, 1, 1))
        return after - before

    def d_y(slab, south, north):
        after = jnp.where(last_row, north, pltpu.roll(slab, ny - 1, 0))
        before = jnp.where(first_row, south, pltpu.roll(slab, 1, 0))
        return after - before

    for load in loads[:4]:
        load.wait()
    for c in range(chunks):

        def edges(i, totals):
            pt, vt, bt = totals
            for j in range(BATCH):
                zl = i * BATCH + j
                z = c * zc + zl
                ps, vs, ws, bs = (p[z + 1], vx[z], vy[z], b[z])
                pt, vt, bt = (pack(pt, ps, zl), pack(vt, vs, zl), pack(bt, bs, zl))
                at = pl.ds(zl, 1)
                ysend[0][0, c, 0, at, :] = ps[0:1]
                ysend[0][0, c, 1, at, :] = ps[1:2]
                ysend[0][0, c, 2, at, :] = ws[0:1]
                ysend[0][0, c, 3, at, :] = bs[0:1]
                ysend[0][1, c, 0, at, :] = ps[ny - 2 : ny - 1]
                ysend[0][1, c, 1, at, :] = ps[ny - 1 : ny]
                ysend[0][1, c, 2, at, :] = ws[ny - 1 : ny]
                ysend[0][1, c, 3, at, :] = bs[ny - 1 : ny]
            return pt, vt, bt

        totals = lax.fori_loop(0, zc // BATCH, edges, (plane, plane, plane))
        for i, total in enumerate(totals):
            xsend[0][c, i] = total
        if c == 0:
            pl.semaphore_wait(barrier, len(peers))
        send(0, c)
    for load in loads[4:]:
        load.wait()

    rup_group, slot_dev, variations = weights.shape
    lanes = weights_got.shape[3]
    group_rows = ngy * CAP
    all_rows = ngx * group_rows

    def weight_block(other):
        block = other * (variations // ngy) // lanes
        return weights.at[:, :, pl.ds(pl.multiple_of(block * lanes, lanes), lanes)]

    def far(kind, k, src, dst):
        axis, size = ("gx", ngx) if kind == 1 else ("gy", ngy)
        return pltpu.make_async_remote_copy(
            src_ref=src,
            dst_ref=dst,
            send_sem=far_send.at[kind, k],
            recv_sem=far_recv.at[kind, k],
            device_id={axis: lax.rem(lax.axis_index(axis) + k, size)},
            device_id_type=pl.DeviceIdType.MESH,
        )

    def rows_of(ref, index, count):
        return ref.at[pl.ds(pl.multiple_of(index * count, count), count)]

    def weights_to(k):
        return far(0, k, weight_block(lax.rem(gy + k, ngy)), weights_got.at[gy])

    def weights_from(k):
        return far(0, k, weight_block(gy), weights_got.at[lax.rem(gy + ngy - k, ngy)])

    def first_to(k):
        src = rows_of(rows_send, lax.rem(gx + k, ngx), group_rows)
        return far(1, k, src, rows_of(rows_group, gx, group_rows))

    def first_from(k):
        src = rows_of(rows_send, gx, group_rows)
        return far(1, k, src, rows_of(rows_group, lax.rem(gx + ngx - k, ngx), group_rows))

    def second_to(k):
        return far(2, k, rows_group, rows_of(rows_out, gy, all_rows))

    def second_from(k):
        return far(2, k, rows_group, rows_of(rows_out, lax.rem(gy + ngy - k, ngy), all_rows))

    for k in range(1, ngy):
        weights_to(k).start()
    own_weights = pltpu.make_async_copy(weight_block(gy), weights_got.at[gy], far_send.at[0, 0])
    own_weights.start()

    square = (per_dev, per_dev)
    eye = lax.broadcasted_iota(jnp.int32, square, 0) == lax.broadcasted_iota(jnp.int32, square, 1)

    def to_row(column):
        return jnp.sum(jnp.where(eye, column, 0.0), axis=0, keepdims=True)

    def to_column(line):
        return jnp.sum(jnp.where(eye, line, 0.0), axis=1, keepdims=True)

    def fill_placing():
        ruptures, slots = listed.shape
        shape = (per_dev, slots)
        own_ids = lax.broadcasted_iota(jnp.int32, shape, 0) + (gx * ngy + gy) * per_dev
        slot_owner = lax.broadcasted_iota(jnp.int32, shape, 1) // slot_dev

        def body(r, best):
            owner = r // rup_group * ngy + slot_owner
            return jnp.where(listed[pl.ds(r, 1), :] == own_ids, owner, best)

        best = lax.fori_loop(0, ruptures, body, jnp.full(shape, -1, jnp.int32))
        target = jnp.max(best.astype(jnp.float32), axis=1, keepdims=True)
        before = lax.broadcasted_iota(jnp.int32, square, 1) < lax.broadcasted_iota(
            jnp.int32, square, 0
        )
        same = (to_row(target) == target) & before
        rank = jnp.sum(jnp.where(same, 1.0, 0.0), axis=1, keepdims=True)
        bucket = to_row(jnp.where(target >= 0.0, target * CAP + rank, -1.0))
        place = lax.broadcasted_iota(jnp.int32, placing.shape, 0).astype(jnp.float32)
        placing[...] = jnp.where(place == bucket, 1.0, 0.0).astype(jnp.bfloat16)

    def halos(r, c):
        def joined(i):
            return jnp.where(lane4 < 2, xrecv[r][0, c, i], xrecv[r][1, c, i])

        def swapped(halo):
            return jnp.where(lane4 == 1, pltpu.roll(halo, nx - 1, 1), pltpu.roll(halo, 1, 1))

        outer, own = (joined(0), xsend[r][c, 0])
        if r == 0:
            vh, bh = (joined(1), joined(2))
            bxh[c] = bh
            vyh[0, c] = yrecv[0][0, c, 2]
            vyh[1, c] = yrecv[0][1, c, 2]
        else:
            vh, bh = (vxh[c], bxh[c])
        slope = jnp.where(
            lane4 == 1,
            pltpu.roll(own, nx - 1, 1) - pltpu.roll(outer, 1, 1),
            pltpu.roll(outer, nx - 1, 1) - pltpu.roll(own, 1, 1),
        )
        vh = vh - bh * slope
        vxh[c] = vh
        hx[0, c] = swapped(outer)
        hx[1, c] = swapped(vh)
        vyh[0, c] = vyh[0, c] - yrecv[0][0, c, 3] * (ysend[r][0, c, 0] - yrecv[r][0, c, 0])
        vyh[1, c] = vyh[1, c] - yrecv[0][1, c, 3] * (yrecv[r][1, c, 1] - ysend[r][1, c, 1])

    def sweep(r, c):
        last = r == STEPS - 1
        n = r + 1

        def body(i, totals):
            pt, wt = totals
            base = i * BATCH
            z0 = c * zc + base
            ps = [p[z0 + 1 + j] for j in range(BATCH + 2)]
            bs = [b[z0 + j] for j in range(BATCH + 1)]
            zs = [vz[z0], vz[z0 + 1]]
            vs, ws, new_p = ([], [], [])
            for j in range(BATCH):
                zl = base + j
                at = pl.ds(zl, 1)
                zs.append(vz[z0 + j + 2] - bs[j + 1] * (ps[j + 2] - ps[j]))
                vs.append(vx[z0 + j] - bs[j] * d_x(ps[j], hx[0, c], zl))
                south, north = (yrecv[r][0, c, 1, at, :], yrecv[r][1, c, 0, at, :])
                ws.append(vy[z0 + j] - bs[j] * d_y(ps[j], south, north))
            for j in range(BATCH):
                zl = base + j
                at = pl.ds(zl, 1)
                spread = d_x(vs[j], hx[1, c], zl) + d_y(ws[j], vyh[0, c, at, :], vyh[1, c, at, :])
                spread = spread + (zs[j + 2] - zs[j])
                mem = m[z0 + j]
                mem = mem - rel[z0 + j] * (mem + stg[z0 + j] * spread)
                m[z0 + j] = mem
                new_p.append(ps[j] - mod[z0 + j] * (spread + mem))
            for j in range(BATCH):
                zl = base + j
                at = pl.ds(zl, 1)
                vz[z0 + j + 2] = zs[j + 2]
                vx[z0 + j] = vs[j]
                vy[z0 + j] = ws[j]
                p[z0 + j + 1] = new_p[j]
                wt = pack(wt, ws[j], zl)
                ysend[n][0, c, 0 if last else 2, at, :] = vs[j][0:1]
                ysend[n][1, c, 0 if last else 2, at, :] = vs[j][ny - 1 : ny]
                if not last:
                    pt = pack(pt, new_p[j], zl)
                    ysend[n][0, c, 0, at, :] = new_p[j][0:1]
                    ysend[n][0, c, 1, at, :] = new_p[j][1:2]
                    ysend[n][1, c, 0, at, :] = new_p[j][ny - 2 : ny - 1]
                    ysend[n][1, c, 1, at, :] = new_p[j][ny - 1 : ny]
            return pt, wt

        pt, wt = lax.fori_loop(0, zc // BATCH, body, (plane, plane))
        if last:
            xsend[n][c, 0] = wt
        else:
            xsend[n][c, 0] = pt
            xsend[n][c, 1] = wt

    fill_placing()
    cells = to_column(cell_row[...].astype(jnp.float32)).astype(jnp.int32)
    cell_z, cell_y, cell_x = (cells // (ny * nx), (cells // nx) % ny, cells % nx)
    patch_lane = lax.broadcasted_iota(jnp.int32, (per_dev, nx), 1)

    def masked(keep, values):
        return jnp.where(keep, values, 0.0)

    def sample_own(n):
        def body(i, carry):
            at = cell[i]
            z, y = (at // (ny * nx), (at // nx) % ny)
            out = pl.ds(i, 1)
            rows_got[0, out, :] = vx[z, pl.ds(jnp.minimum(y + 1, ny - 1), 1), :]
            rows_got[1, out, :] = vx[z, pl.ds(jnp.maximum(y - 1, 0), 1), :]
            rows_got[2, out, :] = vy[z, pl.ds(y, 1), :]
            return carry

        lax.fori_loop(0, per_dev, body, 0, unroll=8)
        along = masked(cell_y < ny - 1, rows_got[0]) - masked(cell_y > 0, rows_got[1])
        across = rows_got[2]
        total = masked(patch_lane == cell_x, along)
        total = total + masked(patch_lane == cell_x + 1, across)
        samples[n - 1] = total - masked(patch_lane == cell_x - 1, across)

    def sample_halo(n):
        which_row, which_pack = (Y_ROWS[n] - 1, X_PACKS[n] - 1)

        def body(i, carry):
            at = cell[i]
            z, y = (at // (ny * nx), (at // nx) % ny)
            c, zl = (z // zc, z % zc)
            out = pl.ds(i, 1)
            rows_got[0, out, :] = yrecv[n][0, c, which_row, pl.ds(zl, 1), :]
            rows_got[1, out, :] = yrecv[n][1, c, which_row, pl.ds(zl, 1), :]
            rows_got[2, out, :] = xrecv[n][0, c, which_pack, pl.ds(y, 1), :]
            rows_got[3, out, :] = xrecv[n][1, c, which_pack, pl.ds(y, 1), :]
            return carry

        lax.fori_loop(0, per_dev, body, 0, unroll=8)
        start = 4 * (cell_z % zc)
        here = patch_lane == cell_x
        total = samples[n - 1]
        total = total + masked(here & (cell_y == ny - 1), rows_got[1])
        total = total - masked(here & (cell_y == 0), rows_got[0])
        total = total + masked((patch_lane == start + 2) & (cell_x == nx - 1), rows_got[3])
        total = total - masked((patch_lane == start + 1) & (cell_x == 0), rows_got[2])
        value = jnp.sum(total, axis=1, keepdims=True)
        spectra_out[...] = spectra_out[...] + value * phase[n - 1 : n, :]

    spectra_out[...] = spectra[...]
    stores = []
    for r in range(STEPS):
        vz[1] = vz[1] - b[0] * (p[2] - p[0])
        for c in range(chunks):
            receive(r, c)
            halos(r, c)
            sweep(r, c)
            send(r + 1, c)
            if r == STEPS - 1:
                at = pl.ds(c * zc, zc)
                pairs = [
                    (vx.at[at], vel_out.at[0, at]),
                    (vy.at[at], vel_out.at[1, at]),
                    (vz.at[pl.ds(1 + c * zc, zc)], vel_out.at[2, at]),
                    (p.at[pl.ds(1 + c * zc, zc)], p_out.at[at]),
                    (m.at[at], m_out.at[at]),
                ]
                for i, (src, dst) in enumerate(pairs):
                    store = pltpu.make_async_copy(src, dst, out_sem.at[c, i])
                    store.start()
                    stores.append(store)
        sample_own(r + 1)
        if r > 0:
            sample_halo(r)
    for c in range(chunks):
        receive(STEPS, c)
    sample_halo(STEPS)
    rows_send[...] = jnp.dot(
        placing[...], spectra_out[...].astype(jnp.bfloat16), preferred_element_type=jnp.float32
    ).astype(jnp.bfloat16)
    for k in range(1, ngx):
        first_to(k).start()
    at = pl.ds(pl.multiple_of(gx * group_rows, group_rows), group_rows)
    rows_group[at, :] = rows_send[at, :]
    for k in range(1, ngx):
        first_from(k).wait_recv()
    for k in range(1, ngy):
        second_to(k).start()
    at = pl.ds(pl.multiple_of(gy * all_rows, all_rows), all_rows)
    rows_out[at, :] = rows_group[...]
    own_weights.wait()
    for k in range(1, ngy):
        weights_from(k).wait_recv()
        weights_to(k).wait_send()
    for k in range(1, ngy):
        second_from(k).wait_recv()
        second_to(k).wait_send()
    for k in range(1, ngx):
        first_to(k).wait_send()
    for r in range(STEPS + 1):
        for c in range(chunks):
            for side in range(4):

                @pl.when(has[side])
                def _():
                    copy_to(r, c, side).wait_send()

    for store in stores:
        store.wait()


def advance(
    velocity, pressure, memory, buoyancy, modulus, relax, strength, spectra, patch_cell, listed, weights
):
    nz, ny, nx = pressure.shape
    per_dev, width = spectra.shape
    zc = nx // 4
    chunks = nz // zc
    ngx, ngy = (lax.axis_size("gx"), lax.axis_size("gy"))
    dims = (nz, ny, nx, chunks, zc, per_dev, ngx, ngy)
    rup_group, slot_dev, variations = weights.shape
    lanes = max(variations // ngy, 128)
    all_rows = ngx * ngy * CAP
    f32 = jnp.float32
    field = lambda planes: pltpu.VMEM((planes, ny, nx), f32)
    rounds = range(STEPS + 1)
    any_spec = pl.BlockSpec(memory_space=pl.ANY)
    vmem_spec = pl.BlockSpec(memory_space=pltpu.VMEM)
    return pl.pallas_call(
        functools.partial(step_kernel, dims),
        out_shape=[
            jax.ShapeDtypeStruct(velocity.shape, f32),
            jax.ShapeDtypeStruct(pressure.shape, f32),
            jax.ShapeDtypeStruct(memory.shape, f32),
            jax.ShapeDtypeStruct(spectra.shape, f32),
            jax.ShapeDtypeStruct((ngy, rup_group, slot_dev, lanes), jnp.bfloat16),
            jax.ShapeDtypeStruct((ngy * all_rows, width), jnp.bfloat16),
        ],
        in_specs=[any_spec] * 7
        + [vmem_spec, pl.BlockSpec(memory_space=pltpu.SMEM)]
        + [vmem_spec] * 4,
        out_specs=[any_spec] * 3 + [vmem_spec] * 3,
        scratch_shapes=[field(nz), field(nz), field(nz + 2), field(nz + 3), field(nz)]
        + [field(nz + 1), field(nz), field(nz), field(nz)]
        + [pltpu.VMEM((2, chunks, Y_ROWS[r], zc, nx), f32) for r in rounds]
        + [pltpu.VMEM((2, chunks, Y_ROWS[r], zc, nx), f32) for r in rounds]
        + [pltpu.VMEM((chunks, X_PACKS[r], ny, nx), f32) for r in rounds]
        + [pltpu.VMEM((2, chunks, X_PACKS[r], ny, nx), f32) for r in rounds]
        + [
            pltpu.VMEM((chunks, ny, nx), f32),
            pltpu.VMEM((chunks, ny, nx), f32),
            pltpu.VMEM((2, chunks, ny, nx), f32),
            pltpu.VMEM((2, chunks, zc, nx), f32),
            pltpu.VMEM((4, per_dev, nx), f32),
            pltpu.VMEM((STEPS, per_dev, nx), f32),
            pltpu.VMEM((all_rows, per_dev), jnp.bfloat16),
            pltpu.VMEM((all_rows, width), jnp.bfloat16),
            pltpu.VMEM((all_rows, width), jnp.bfloat16),
            pltpu.SemaphoreType.DMA((9,)),
            pltpu.SemaphoreType.DMA((chunks, 5)),
            pltpu.SemaphoreType.DMA((STEPS + 1, chunks, 4)),
            pltpu.SemaphoreType.DMA((STEPS + 1, chunks, 4)),
            pltpu.SemaphoreType.DMA((3, max(ngx, ngy))),
            pltpu.SemaphoreType.DMA((3, max(ngx, ngy))),
        ],
        compiler_params=pltpu.CompilerParams(collective_id=0, has_side_effects=True),
    )(
        velocity,
        pressure,
        memory,
        buoyancy,
        modulus,
        relax,
        strength,
        spectra,
        patch_cell,
        patch_cell.reshape(1, -1),
        phase_rows(width // 2),
        listed,
        weights,
    )


def per_device(
    velocity,
    pressure,
    memory,
    buoyancy,
    modulus,
    relax,
    strength,
    spectra,
    patch_cell,
    rupture_patches,
    slip_weights,
):
    velocity_out, pressure, memory, spectra, weights, rows = advance(
        velocity,
        pressure,
        memory,
        buoyancy,
        modulus,
        relax,
        strength,
        spectra,
        patch_cell,
        rupture_patches,
        slip_weights,
    )
    groups_x, groups_y = (lax.axis_size("gx"), lax.axis_size("gy"))
    per_dev = spectra.shape[0]
    rup_group, slot_dev, variations = slip_weights.shape
    ids = lax.dynamic_slice_in_dim(
        rupture_patches, lax.axis_index("gx") * rup_group, rup_group, axis=0
    )
    ids = ids.reshape(rup_group, groups_y, slot_dev).transpose(1, 0, 2).reshape(groups_y, -1)
    source = ids // per_dev
    earlier = (ids[:, None, :] < ids[:, :, None]) & (source[:, None, :] == source[:, :, None])
    rank = jnp.sum((earlier & (ids[:, None, :] >= 0)).astype(jnp.int32), axis=2)
    owner = jnp.arange(groups_y, dtype=jnp.int32)[:, None]
    block = source % groups_y * groups_x + source // groups_y
    row = jnp.where(ids >= 0, (block * groups_y + owner) * CAP + rank, -1)
    chosen = (row[:, :, None] == jnp.arange(rows.shape[0], dtype=jnp.int32)).astype(jnp.bfloat16)
    slot_spectra = jnp.einsum("gkq,qf->gkf", chosen, rows, preferred_element_type=jnp.float32)
    slot_spectra = slot_spectra.astype(jnp.bfloat16).reshape(groups_y, rup_group, slot_dev, -1)
    share = variations // groups_y
    start = lax.axis_index("gy") * share % weights.shape[3]
    own = lax.dynamic_slice_in_dim(weights, start, share, axis=3)
    slip = jnp.einsum("grsv,grsf->rvf", own, slot_spectra, preferred_element_type=jnp.float32)
    return (velocity_out, pressure, memory, spectra, slip)


def solution(mesh):
    in_specs = (
        P(None, None, "gy", "gx"),
        P(None, "gy", "gx"),
        P(None, "gy", "gx"),
        P(None, "gy", "gx"),
        P(None, "gy", "gx"),
        P(None, "gy", "gx"),
        P(None, "gy", "gx"),
        P(("gx", "gy"), None),
        P(("gx", "gy")),
        P(),
        P("gx", "gy", None),
    )
    out_specs = (
        P(None, None, "gy", "gx"),
        P(None, "gy", "gx"),
        P(None, "gy", "gx"),
        P(("gx", "gy"), None),
        P("gx", "gy", None),
    )
    return jax.shard_map(
        per_device, mesh=mesh, in_specs=in_specs, out_specs=out_specs, check_vma=False
    )
```

```python
import functools

import jax
import jax.numpy as jnp
import numpy as np
from jax import lax
from jax.experimental import pallas as pl
from jax.experimental.pallas import tpu as pltpu
from jax.sharding import PartitionSpec as P

STEPS = 4
CAP = 2
BATCH = 8


def phase_rows(freqs):
    angle = np.pi * (np.arange(freqs) + 0.5) / freqs
    rows = [np.concatenate([np.cos(angle * n), -np.sin(angle * n)]) for n in range(1, STEPS + 1)]
    return jnp.asarray(np.stack(rows).astype(np.float32))


Y_ROWS = [4] + [3] * (STEPS - 1) + [1]
X_PACKS = [3] + [2] * (STEPS - 1) + [1]


def quotient(value, size):
    if size & (size - 1):
        return lax.div(value, jnp.full_like(value, size))
    return lax.shift_right_logical(value, jnp.full_like(value, size.bit_length() - 1))


def remainder(value, size):
    if size & (size - 1):
        return lax.rem(value, jnp.full_like(value, size))
    return value & (size - 1)


def step_kernel(dims, *refs):
    nz, ny, nx, chunks, zc, per_dev, ngx, ngy = dims
    refs = list(refs)
    take = lambda count: [refs.pop(0) for _ in range(count)]
    vel_in, p_in, m_in, b_in, mod_in, rel_in, str_in, spectra, cell, cell_row, phase = take(11)
    listed, weights = take(2)
    vel_out, p_out, m_out, spectra_out, weights_got, rows_out = take(6)
    vx, vy, vz, p, m, b, mod, rel, stg = take(9)
    ysend, yrecv = (take(STEPS + 1), take(STEPS + 1))
    xsend, xrecv = (take(STEPS + 1), take(STEPS + 1))
    vxh, bxh, hx, vyh, rows_got, samples = take(6)
    placing, rows_send, rows_group = take(3)
    in_sem, out_sem, send_sem, recv_sem, far_send, far_recv = take(6)

    gx, gy = (lax.axis_index("gx"), lax.axis_index("gy"))
    has = [gy > 0, gy < ngy - 1, gx > 0, gx < ngx - 1]
    peer = [{"gy": gy - 1}, {"gy": gy + 1}, {"gx": gx - 1}, {"gx": gx + 1}]

    loads = [
        pltpu.make_async_copy(src, dst, in_sem.at[i])
        for i, (src, dst) in enumerate(
            [
                (p_in, p.at[pl.ds(1, nz)]),
                (b_in, b.at[pl.ds(0, nz)]),
                (vel_in.at[0], vx),
                (vel_in.at[1], vy),
                (vel_in.at[2], vz.at[pl.ds(1, nz)]),
                (rel_in, rel),
                (m_in, m),
                (str_in, stg),
                (mod_in, mod),
            ]
        )
    ]
    for load in loads:
        load.start()

    along_gx = [lax.rem(gx + k, ngx) for k in range(1, ngx)]
    along_gy = [lax.rem(gy + k, ngy) for k in range(1, ngy)]
    peers = [{"gx": other} for other in along_gx] + [{"gy": other} for other in along_gy]
    barrier = pltpu.get_barrier_semaphore()
    for other in peers:
        pl.semaphore_signal(
            barrier, inc=1, device_id=other, device_id_type=pl.DeviceIdType.MESH
        )

    plane = jnp.zeros((ny, nx), jnp.float32)
    p[0] = plane
    p[nz + 1] = plane
    p[nz + 2] = plane
    vz[0] = plane
    vz[nz + 1] = plane
    b[nz] = plane
    for side in range(4):

        @pl.when(jnp.logical_not(has[side]))
        def _():
            for r in range(STEPS + 1):
                if side < 2:
                    yrecv[r][side] = jnp.zeros(yrecv[r].shape[1:], jnp.float32)
                else:
                    xrecv[r][side - 2] = jnp.zeros(xrecv[r].shape[1:], jnp.float32)

    def copy_to(r, c, side):
        slot = side % 2
        if side < 2:
            src, dst = (ysend[r].at[slot, c], yrecv[r].at[1 - slot, c])
        else:
            src, dst = (xsend[r].at[c], xrecv[r].at[1 - slot, c])
        return pltpu.make_async_remote_copy(
            src_ref=src,
            dst_ref=dst,
            send_sem=send_sem.at[r, c, side],
            recv_sem=recv_sem.at[r, c, side - side % 2 + 1 - slot],
            device_id=peer[side],
            device_id_type=pl.DeviceIdType.MESH,
        )

    def copy_from(r, c, side):
        slot = side % 2
        if side < 2:
            src, dst = (ysend[r].at[slot, c], yrecv[r].at[slot, c])
        else:
            src, dst = (xsend[r].at[c], xrecv[r].at[slot, c])
        return pltpu.make_async_remote_copy(
            src_ref=src,
            dst_ref=dst,
            send_sem=send_sem.at[r, c, side],
            recv_sem=recv_sem.at[r, c, side],
            device_id=peer[side],
            device_id_type=pl.DeviceIdType.MESH,
        )

    def send(r, c):
        for side in range(4):

            @pl.when(has[side])
            def _():
                copy_to(r, c, side).start()

    def receive(r, c):
        for side in range(4):

            @pl.when(has[side])
            def _():
                copy_from(r, c, side).wait_recv()

    lane = lax.broadcasted_iota(jnp.int32, (ny, nx), 1)
    row = lax.broadcasted_iota(jnp.int32, (ny, nx), 0)
    quad, lane4 = (quotient(lane, 4), remainder(lane, 4))
    last_lane, first_lane = (lane == nx - 1, lane == 0)
    last_row, first_row = (row == ny - 1, row == 0)

    def pack(total, slab, zl):
        return jnp.where(quad == zl, pltpu.roll(slab, 4 * zl + 2, 1), total)

    def d_x(slab, halo, zl):
        ends = pltpu.roll(halo, nx - 2 - 4 * zl, 1)
        after = jnp.where(last_lane, ends, pltpu.roll(slab, nx - 1, 1))
        before = jnp.where(first_lane, ends, pltpu.roll(slab, 1, 1))
        return after - before

    def d_y(slab, south, north):
        after = jnp.where(last_row, north, pltpu.roll(slab, ny - 1, 0))
        before = jnp.where(first_row, south, pltpu.roll(slab, 1, 0))
        return after - before

    for load in loads[:4]:
        load.wait()
    for c in range(chunks):

        def edges(i, totals):
            pt, vt, bt = totals
            for j in range(BATCH):
                zl = i * BATCH + j
                z = c * zc + zl
                ps, vs, ws, bs = (p[z + 1], vx[z], vy[z], b[z])
                pt, vt, bt = (pack(pt, ps, zl), pack(vt, vs, zl), pack(bt, bs, zl))
                at = pl.ds(zl, 1)
                ysend[0][0, c, 0, at, :] = ps[0:1]
                ysend[0][0, c, 1, at, :] = ps[1:2]
                ysend[0][0, c, 2, at, :] = ws[0:1]
                ysend[0][0, c, 3, at, :] = bs[0:1]
                ysend[0][1, c, 0, at, :] = ps[ny - 2 : ny - 1]
                ysend[0][1, c, 1, at, :] = ps[ny - 1 : ny]
                ysend[0][1, c, 2, at, :] = ws[ny - 1 : ny]
                ysend[0][1, c, 3, at, :] = bs[ny - 1 : ny]
            return pt, vt, bt

        totals = lax.fori_loop(0, zc // BATCH, edges, (plane, plane, plane))
        for i, total in enumerate(totals):
            xsend[0][c, i] = total
        if c == 0:
            pl.semaphore_wait(barrier, len(peers))
        send(0, c)
    for load in loads[4:]:
        load.wait()

    rup_group, slot_dev, variations = weights.shape
    lanes = weights_got.shape[3]
    group_rows = ngy * CAP
    all_rows = ngx * group_rows

    def weight_block(other):
        block = other * (variations // ngy) // lanes
        return weights.at[:, :, pl.ds(pl.multiple_of(block * lanes, lanes), lanes)]

    def far(kind, k, src, dst):
        axis, size = ("gx", ngx) if kind == 1 else ("gy", ngy)
        return pltpu.make_async_remote_copy(
            src_ref=src,
            dst_ref=dst,
            send_sem=far_send.at[kind, k],
            recv_sem=far_recv.at[kind, k],
            device_id={axis: lax.rem(lax.axis_index(axis) + k, size)},
            device_id_type=pl.DeviceIdType.MESH,
        )

    def rows_of(ref, index, count):
        return ref.at[pl.ds(pl.multiple_of(index * count, count), count)]

    def weights_to(k):
        return far(0, k, weight_block(lax.rem(gy + k, ngy)), weights_got.at[gy])

    def weights_from(k):
        return far(0, k, weight_block(gy), weights_got.at[lax.rem(gy + ngy - k, ngy)])

    def first_to(k):
        src = rows_of(rows_send, lax.rem(gx + k, ngx), group_rows)
        return far(1, k, src, rows_of(rows_group, gx, group_rows))

    def first_from(k):
        src = rows_of(rows_send, gx, group_rows)
        return far(1, k, src, rows_of(rows_group, lax.rem(gx + ngx - k, ngx), group_rows))

    def second_to(k):
        return far(2, k, rows_group, rows_of(rows_out, gy, all_rows))

    def second_from(k):
        return far(2, k, rows_group, rows_of(rows_out, lax.rem(gy + ngy - k, ngy), all_rows))

    for k in range(1, ngy):
        weights_to(k).start()
    own_weights = pltpu.make_async_copy(weight_block(gy), weights_got.at[gy], far_send.at[0, 0])
    own_weights.start()

    square = (per_dev, per_dev)
    eye = lax.broadcasted_iota(jnp.int32, square, 0) == lax.broadcasted_iota(jnp.int32, square, 1)

    def to_row(column):
        return jnp.sum(jnp.where(eye, column, 0.0), axis=0, keepdims=True)

    def to_column(line):
        return jnp.sum(jnp.where(eye, line, 0.0), axis=1, keepdims=True)

    def fill_placing():
        ruptures, slots = listed.shape
        shape = (per_dev, slots)
        own_ids = lax.broadcasted_iota(jnp.int32, shape, 0) + (gx * ngy + gy) * per_dev
        slot_owner = quotient(lax.broadcasted_iota(jnp.int32, shape, 1), slot_dev)

        def body(r, best):
            owner = quotient(r, rup_group) * ngy + slot_owner
            return jnp.where(listed[pl.ds(r, 1), :] == own_ids, owner, best)

        best = lax.fori_loop(0, ruptures, body, jnp.full(shape, -1, jnp.int32))
        target = jnp.max(best.astype(jnp.float32), axis=1, keepdims=True)
        before = lax.broadcasted_iota(jnp.int32, square, 1) < lax.broadcasted_iota(
            jnp.int32, square, 0
        )
        same = (to_row(target) == target) & before
        rank = jnp.sum(jnp.where(same, 1.0, 0.0), axis=1, keepdims=True)
        bucket = to_row(jnp.where(target >= 0.0, target * CAP + rank, -1.0))
        place = lax.broadcasted_iota(jnp.int32, placing.shape, 0).astype(jnp.float32)
        placing[...] = jnp.where(place == bucket, 1.0, 0.0).astype(jnp.bfloat16)

    def halos(r, c):
        def joined(i):
            return jnp.where(lane4 < 2, xrecv[r][0, c, i], xrecv[r][1, c, i])

        def swapped(halo):
            return jnp.where(lane4 == 1, pltpu.roll(halo, nx - 1, 1), pltpu.roll(halo, 1, 1))

        outer, own = (joined(0), xsend[r][c, 0])
        if r == 0:
            vh, bh = (joined(1), joined(2))
            bxh[c] = bh
            vyh[0, c] = yrecv[0][0, c, 2]
            vyh[1, c] = yrecv[0][1, c, 2]
        else:
            vh, bh = (vxh[c], bxh[c])
        slope = jnp.where(
            lane4 == 1,
            pltpu.roll(own, nx - 1, 1) - pltpu.roll(outer, 1, 1),
            pltpu.roll(outer, nx - 1, 1) - pltpu.roll(own, 1, 1),
        )
        vh = vh - bh * slope
        vxh[c] = vh
        hx[0, c] = swapped(outer)
        hx[1, c] = swapped(vh)
        vyh[0, c] = vyh[0, c] - yrecv[0][0, c, 3] * (ysend[r][0, c, 0] - yrecv[r][0, c, 0])
        vyh[1, c] = vyh[1, c] - yrecv[0][1, c, 3] * (yrecv[r][1, c, 1] - ysend[r][1, c, 1])

    def sweep(r, c):
        last = r == STEPS - 1
        n = r + 1

        def body(i, totals):
            pt, wt = totals
            base = i * BATCH
            z0 = c * zc + base
            ps = [p[z0 + 1 + j] for j in range(BATCH + 2)]
            bs = [b[z0 + j] for j in range(BATCH + 1)]
            zs = [vz[z0], vz[z0 + 1]]
            vs, ws, new_p = ([], [], [])
            for j in range(BATCH):
                zl = base + j
                at = pl.ds(zl, 1)
                zs.append(vz[z0 + j + 2] - bs[j + 1] * (ps[j + 2] - ps[j]))
                vs.append(vx[z0 + j] - bs[j] * d_x(ps[j], hx[0, c], zl))
                south, north = (yrecv[r][0, c, 1, at, :], yrecv[r][1, c, 0, at, :])
                ws.append(vy[z0 + j] - bs[j] * d_y(ps[j], south, north))
            for j in range(BATCH):
                zl = base + j
                at = pl.ds(zl, 1)
                spread = d_x(vs[j], hx[1, c], zl) + d_y(ws[j], vyh[0, c, at, :], vyh[1, c, at, :])
                spread = spread + (zs[j + 2] - zs[j])
                mem = m[z0 + j]
                mem = mem - rel[z0 + j] * (mem + stg[z0 + j] * spread)
                m[z0 + j] = mem
                new_p.append(ps[j] - mod[z0 + j] * (spread + mem))
            for j in range(BATCH):
                zl = base + j
                at = pl.ds(zl, 1)
                vz[z0 + j + 2] = zs[j + 2]
                vx[z0 + j] = vs[j]
                vy[z0 + j] = ws[j]
                p[z0 + j + 1] = new_p[j]
                wt = pack(wt, ws[j], zl)
                ysend[n][0, c, 0 if last else 2, at, :] = vs[j][0:1]
                ysend[n][1, c, 0 if last else 2, at, :] = vs[j][ny - 1 : ny]
                if not last:
                    pt = pack(pt, new_p[j], zl)
                    ysend[n][0, c, 0, at, :] = new_p[j][0:1]
                    ysend[n][0, c, 1, at, :] = new_p[j][1:2]
                    ysend[n][1, c, 0, at, :] = new_p[j][ny - 2 : ny - 1]
                    ysend[n][1, c, 1, at, :] = new_p[j][ny - 1 : ny]
            return pt, wt

        pt, wt = lax.fori_loop(0, zc // BATCH, body, (plane, plane))
        if last:
            xsend[n][c, 0] = wt
        else:
            xsend[n][c, 0] = pt
            xsend[n][c, 1] = wt

    fill_placing()
    cells = to_column(cell_row[...].astype(jnp.float32)).astype(jnp.int32)
    cell_z, cell_x = (quotient(cells, ny * nx), remainder(cells, nx))
    cell_y = remainder(quotient(cells, nx), ny)
    patch_lane = lax.broadcasted_iota(jnp.int32, (per_dev, nx), 1)

    def masked(keep, values):
        return jnp.where(keep, values, 0.0)

    def sample_own(n):
        def body(i, carry):
            at = cell[i]
            z, y = (quotient(at, ny * nx), remainder(quotient(at, nx), ny))
            out = pl.ds(i, 1)
            rows_got[0, out, :] = vx[z, pl.ds(jnp.minimum(y + 1, ny - 1), 1), :]
            rows_got[1, out, :] = vx[z, pl.ds(jnp.maximum(y - 1, 0), 1), :]
            rows_got[2, out, :] = vy[z, pl.ds(y, 1), :]
            return carry

        lax.fori_loop(0, per_dev, body, 0, unroll=8)
        along = masked(cell_y < ny - 1, rows_got[0]) - masked(cell_y > 0, rows_got[1])
        across = rows_got[2]
        total = masked(patch_lane == cell_x, along)
        total = total + masked(patch_lane == cell_x + 1, across)
        samples[n - 1] = total - masked(patch_lane == cell_x - 1, across)

    def sample_halo(n):
        which_row, which_pack = (Y_ROWS[n] - 1, X_PACKS[n] - 1)

        def body(i, carry):
            at = cell[i]
            z, y = (quotient(at, ny * nx), remainder(quotient(at, nx), ny))
            c, zl = (quotient(z, zc), remainder(z, zc))
            out = pl.ds(i, 1)
            rows_got[0, out, :] = yrecv[n][0, c, which_row, pl.ds(zl, 1), :]
            rows_got[1, out, :] = yrecv[n][1, c, which_row, pl.ds(zl, 1), :]
            rows_got[2, out, :] = xrecv[n][0, c, which_pack, pl.ds(y, 1), :]
            rows_got[3, out, :] = xrecv[n][1, c, which_pack, pl.ds(y, 1), :]
            return carry

        lax.fori_loop(0, per_dev, body, 0, unroll=8)
        start = 4 * remainder(cell_z, zc)
        here = patch_lane == cell_x
        total = samples[n - 1]
        total = total + masked(here & (cell_y == ny - 1), rows_got[1])
        total = total - masked(here & (cell_y == 0), rows_got[0])
        total = total + masked((patch_lane == start + 2) & (cell_x == nx - 1), rows_got[3])
        total = total - masked((patch_lane == start + 1) & (cell_x == 0), rows_got[2])
        value = jnp.sum(total, axis=1, keepdims=True)
        spectra_out[...] = spectra_out[...] + value * phase[n - 1 : n, :]

    spectra_out[...] = spectra[...]
    stores = []
    for r in range(STEPS):
        vz[1] = vz[1] - b[0] * (p[2] - p[0])
        for c in range(chunks):
            receive(r, c)
            halos(r, c)
            sweep(r, c)
            send(r + 1, c)
            if r == STEPS - 1:
                at = pl.ds(c * zc, zc)
                pairs = [
                    (vx.at[at], vel_out.at[0, at]),
                    (vy.at[at], vel_out.at[1, at]),
                    (vz.at[pl.ds(1 + c * zc, zc)], vel_out.at[2, at]),
                    (p.at[pl.ds(1 + c * zc, zc)], p_out.at[at]),
                    (m.at[at], m_out.at[at]),
                ]
                for i, (src, dst) in enumerate(pairs):
                    store = pltpu.make_async_copy(src, dst, out_sem.at[c, i])
                    store.start()
                    stores.append(store)
        sample_own(r + 1)
        if r > 0:
            sample_halo(r)
    for c in range(chunks):
        receive(STEPS, c)
    sample_halo(STEPS)
    rows_send[...] = jnp.dot(
        placing[...], spectra_out[...].astype(jnp.bfloat16), preferred_element_type=jnp.float32
    ).astype(jnp.bfloat16)
    for k in range(1, ngx):
        first_to(k).start()
    at = pl.ds(pl.multiple_of(gx * group_rows, group_rows), group_rows)
    rows_group[at, :] = rows_send[at, :]
    for k in range(1, ngx):
        first_from(k).wait_recv()
    for k in range(1, ngy):
        second_to(k).start()
    at = pl.ds(pl.multiple_of(gy * all_rows, all_rows), all_rows)
    rows_out[at, :] = rows_group[...]
    own_weights.wait()
    for k in range(1, ngy):
        weights_from(k).wait_recv()
        weights_to(k).wait_send()
    for k in range(1, ngy):
        second_from(k).wait_recv()
        second_to(k).wait_send()
    for k in range(1, ngx):
        first_to(k).wait_send()
    for r in range(STEPS + 1):
        for c in range(chunks):
            for side in range(4):

                @pl.when(has[side])
                def _():
                    copy_to(r, c, side).wait_send()

    for store in stores:
        store.wait()


def advance(
    velocity, pressure, memory, buoyancy, modulus, relax, strength, spectra, patch_cell, listed, weights
):
    nz, ny, nx = pressure.shape
    per_dev, width = spectra.shape
    zc = nx // 4
    chunks = nz // zc
    ngx, ngy = (lax.axis_size("gx"), lax.axis_size("gy"))
    dims = (nz, ny, nx, chunks, zc, per_dev, ngx, ngy)
    rup_group, slot_dev, variations = weights.shape
    lanes = max(variations // ngy, 128)
    all_rows = ngx * ngy * CAP
    f32 = jnp.float32
    field = lambda planes: pltpu.VMEM((planes, ny, nx), f32)
    rounds = range(STEPS + 1)
    any_spec = pl.BlockSpec(memory_space=pl.ANY)
    vmem_spec = pl.BlockSpec(memory_space=pltpu.VMEM)
    return pl.pallas_call(
        functools.partial(step_kernel, dims),
        out_shape=[
            jax.ShapeDtypeStruct(velocity.shape, f32),
            jax.ShapeDtypeStruct(pressure.shape, f32),
            jax.ShapeDtypeStruct(memory.shape, f32),
            jax.ShapeDtypeStruct(spectra.shape, f32),
            jax.ShapeDtypeStruct((ngy, rup_group, slot_dev, lanes), jnp.bfloat16),
            jax.ShapeDtypeStruct((ngy * all_rows, width), jnp.bfloat16),
        ],
        in_specs=[any_spec] * 7
        + [vmem_spec, pl.BlockSpec(memory_space=pltpu.SMEM)]
        + [vmem_spec] * 4,
        out_specs=[any_spec] * 3 + [vmem_spec] * 3,
        scratch_shapes=[field(nz), field(nz), field(nz + 2), field(nz + 3), field(nz)]
        + [field(nz + 1), field(nz), field(nz), field(nz)]
        + [pltpu.VMEM((2, chunks, Y_ROWS[r], zc, nx), f32) for r in rounds]
        + [pltpu.VMEM((2, chunks, Y_ROWS[r], zc, nx), f32) for r in rounds]
        + [pltpu.VMEM((chunks, X_PACKS[r], ny, nx), f32) for r in rounds]
        + [pltpu.VMEM((2, chunks, X_PACKS[r], ny, nx), f32) for r in rounds]
        + [
            pltpu.VMEM((chunks, ny, nx), f32),
            pltpu.VMEM((chunks, ny, nx), f32),
            pltpu.VMEM((2, chunks, ny, nx), f32),
            pltpu.VMEM((2, chunks, zc, nx), f32),
            pltpu.VMEM((4, per_dev, nx), f32),
            pltpu.VMEM((STEPS, per_dev, nx), f32),
            pltpu.VMEM((all_rows, per_dev), jnp.bfloat16),
            pltpu.VMEM((all_rows, width), jnp.bfloat16),
            pltpu.VMEM((all_rows, width), jnp.bfloat16),
            pltpu.SemaphoreType.DMA((9,)),
            pltpu.SemaphoreType.DMA((chunks, 5)),
            pltpu.SemaphoreType.DMA((STEPS + 1, chunks, 4)),
            pltpu.SemaphoreType.DMA((STEPS + 1, chunks, 4)),
            pltpu.SemaphoreType.DMA((3, max(ngx, ngy))),
            pltpu.SemaphoreType.DMA((3, max(ngx, ngy))),
        ],
        compiler_params=pltpu.CompilerParams(collective_id=0, has_side_effects=True),
    )(
        velocity,
        pressure,
        memory,
        buoyancy,
        modulus,
        relax,
        strength,
        spectra,
        patch_cell,
        patch_cell.reshape(1, -1),
        phase_rows(width // 2),
        listed,
        weights,
    )


def per_device(
    velocity,
    pressure,
    memory,
    buoyancy,
    modulus,
    relax,
    strength,
    spectra,
    patch_cell,
    rupture_patches,
    slip_weights,
):
    velocity_out, pressure, memory, spectra, weights, rows = advance(
        velocity,
        pressure,
        memory,
        buoyancy,
        modulus,
        relax,
        strength,
        spectra,
        patch_cell,
        rupture_patches,
        slip_weights,
    )
    groups_x, groups_y = (lax.axis_size("gx"), lax.axis_size("gy"))
    per_dev = spectra.shape[0]
    rup_group, slot_dev, variations = slip_weights.shape
    ids = lax.dynamic_slice_in_dim(
        rupture_patches, lax.axis_index("gx") * rup_group, rup_group, axis=0
    )
    ids = ids.reshape(rup_group, groups_y, slot_dev).transpose(1, 0, 2).reshape(groups_y, -1)
    source = ids // per_dev
    earlier = (ids[:, None, :] < ids[:, :, None]) & (source[:, None, :] == source[:, :, None])
    rank = jnp.sum((earlier & (ids[:, None, :] >= 0)).astype(jnp.int32), axis=2)
    owner = jnp.arange(groups_y, dtype=jnp.int32)[:, None]
    block = source % groups_y * groups_x + source // groups_y
    row = jnp.where(ids >= 0, (block * groups_y + owner) * CAP + rank, -1)
    chosen = (row[:, :, None] == jnp.arange(rows.shape[0], dtype=jnp.int32)).astype(jnp.bfloat16)
    slot_spectra = jnp.einsum("gkq,qf->gkf", chosen, rows, preferred_element_type=jnp.float32)
    slot_spectra = slot_spectra.astype(jnp.bfloat16).reshape(groups_y, rup_group, slot_dev, -1)
    share = variations // groups_y
    start = lax.axis_index("gy") * share % weights.shape[3]
    own = lax.dynamic_slice_in_dim(weights, start, share, axis=3)
    slip = jnp.einsum("grsv,grsf->rvf", own, slot_spectra, preferred_element_type=jnp.float32)
    return (velocity_out, pressure, memory, spectra, slip)


def solution(mesh):
    in_specs = (
        P(None, None, "gy", "gx"),
        P(None, "gy", "gx"),
        P(None, "gy", "gx"),
        P(None, "gy", "gx"),
        P(None, "gy", "gx"),
        P(None, "gy", "gx"),
        P(None, "gy", "gx"),
        P(("gx", "gy"), None),
        P(("gx", "gy")),
        P(),
        P("gx", "gy", None),
    )
    out_specs = (
        P(None, None, "gy", "gx"),
        P(None, "gy", "gx"),
        P(None, "gy", "gx"),
        P(("gx", "gy"), None),
        P("gx", "gy", None),
    )
    return jax.shard_map(
        per_device, mesh=mesh, in_specs=in_specs, out_specs=out_specs, check_vma=False
    )
```
